512 devices in a mesh: wide: 32 (over x, z_hi, core), narrow: 16 (over z_lo, y).
Axes of the slice: x: 4, y: 4, z: 16 (z_hi: 4, z_lo: 4; z = z_hi * 4 + z_lo), core: 2. Of those that a mesh axis runs over, the one named last changes fastest.
Arguments:
- local_slopes: float32 [512, 512, 128], P(('wide', 'narrow')), may hold values from -0.25 to 0.25
- global_slopes: float32 [512, 512, 1024], P(('wide', 'narrow')), may hold values from -0.25 to 0.25
- residuals: float32 [512, 512], P(('wide', 'narrow')), may hold values from -6 to 6
- weights: float32 [512, 512], P(('wide', 'narrow')), may hold values from 0.1 to 10
- track_slot_count: int32 [512], P(('wide', 'narrow')), may hold values from 64 to 512
- windows: int32 [512], P(('wide', 'narrow')), may hold values from 0 to 3
Outputs:
- normal_matrix: float32 [4, 1024, 1024], P(None, 'narrow', 'wide')
- normal_rhs: float32 [4, 1024], P(None, 'narrow')
The draws below stay inside these ranges and needn't reach their ends.
All inputs are finite; a program needn't handle non-finite values.
Results may differ from the reference program's by a relative error of at most 0.0003.
Values sent between devices are 32-bit elements; how exact they have to be, the bound alone decides.
No kernel may reach another device: no remote copies, remote signals or barrier semaphores. Data moves between devices by JAX's collectives and lax.ppermute only.
A program may use at most 64 MiB of HBM per device.

```python
import math
import jax
import jax.numpy as jnp
from jax import lax

WINDOW_PARAMS = 1024
LOCAL_PARAMS = 128
MEASURE_SLOTS = 512
NWIN = 4
TRACK_BUNDLES = 512


def set_ends(drawn, own_key, low, top_value):
    index_at = [jax.random.randint(jax.random.fold_in(own_key, axis), (), 0, length) for axis, length in enumerate(drawn.shape)]
    main_axis = drawn.shape.index(max(drawn.shape))
    next_to = index_at[:main_axis] + [(index_at[main_axis] + 1) % drawn.shape[main_axis]] + index_at[main_axis + 1:]
    return drawn.at[tuple(index_at)].set(low).at[tuple(next_to)].set(top_value)


def levels(stream_key, extent, shards, least, top_value):
    level = 1.0
    for dim, shards_of in shards:
        draws = jax.random.uniform(jax.random.fold_in(jax.random.fold_in(stream_key, 6), dim), (shards_of,), jnp.float32, least / len(shards), top_value / len(shards))
        level = level * jnp.repeat(jnp.exp(draws), extent[dim] // shards_of).reshape((-1,) + (1,) * (len(extent) - 1 - dim))
    return level


def bell_draw(key, dims, scale, most, shards=(), held_as=jnp.bfloat16):
    entries = scale * jax.random.normal(key, dims, jnp.float32)
    if shards:
        entries = entries * levels(key, dims, shards, -0.22, 0.18)
    return jnp.clip(entries, -most, most).astype(held_as)


def setup_inputs(seed: int = 0) -> dict:
    arg_keys = jax.random.split(jax.random.key(seed), 7)
    local_slopes = bell_draw(arg_keys[0], (TRACK_BUNDLES, MEASURE_SLOTS, LOCAL_PARAMS), MEASURE_SLOTS ** -0.5, 0.25, ((0, 512),), jnp.float32)
    global_slopes = bell_draw(arg_keys[1], (TRACK_BUNDLES, MEASURE_SLOTS, WINDOW_PARAMS), MEASURE_SLOTS ** -0.5, 0.25, ((0, 512),), jnp.float32)
    residuals = bell_draw(arg_keys[2], (TRACK_BUNDLES, MEASURE_SLOTS), 1.0, 6.0, ((0, 512),), jnp.float32)
    weights = jnp.clip(jnp.exp(math.log(10.0) - 4.6051702 * jax.random.uniform(arg_keys[3], (TRACK_BUNDLES, MEASURE_SLOTS), jnp.float32) ** levels(arg_keys[3], (TRACK_BUNDLES, MEASURE_SLOTS), ((0, 512),), -0.2, 0.2)), 0.1, 10.0)
    track_slot_count = set_ends(jax.random.randint(arg_keys[4], (TRACK_BUNDLES,), MEASURE_SLOTS // 8, MEASURE_SLOTS + 1), jax.random.fold_in(arg_keys[4], 1), MEASURE_SLOTS // 8, MEASURE_SLOTS).astype(jnp.int32)
    windows = set_ends(jax.random.randint(arg_keys[5], (TRACK_BUNDLES,), 0, NWIN), jax.random.fold_in(arg_keys[5], 1), 0, NWIN - 1).astype(jnp.int32)
    return {"local_slopes": local_slopes, "global_slopes": global_slopes, "residuals": residuals, "weights": weights, "track_slot_count": track_slot_count, "windows": windows}


def tdot(left, right):
    return lax.dot_general(left.astype(jnp.float32), right.astype(jnp.float32), (((0,), (0,)), ((), ())), precision=lax.Precision.HIGHEST, preferred_element_type=jnp.float32)

def reference(local_slopes, global_slopes, residuals, weights, track_slot_count, windows):
    slot_entries = jnp.arange(MEASURE_SLOTS, dtype=jnp.int32)

    def one_bundle(carry, items):
        matrix, rhs = carry
        local_b, global_b, resid_b, weight_b, count_b, window_b = items
        live = jnp.where(slot_entries < count_b, weight_b, jnp.float32(0.0))
        wl = local_b * live[:, None]
        wg = global_b * live[:, None]
        curv = tdot(wl, local_b) + jnp.eye(LOCAL_PARAMS, dtype=jnp.float32)
        coupling = tdot(wl, global_b)
        lr = tdot(wl, resid_b[:, None])
        gram = tdot(wg, global_b)
        gr = tdot(wg, resid_b[:, None])[:, 0]
        factor = jnp.linalg.cholesky(curv)
        solved = jax.scipy.linalg.cho_solve((factor, True), jnp.concatenate([coupling, lr], axis=1))
        schur = gram - tdot(coupling, solved[:, :WINDOW_PARAMS])
        srhs = gr - tdot(coupling, solved[:, WINDOW_PARAMS:])[:, 0]
        picks = (jnp.arange(NWIN, dtype=jnp.int32) == window_b).astype(jnp.float32)
        matrix = matrix + picks[:, None, None] * schur[None]
        rhs = rhs + picks[:, None] * srhs[None]
        return ((matrix, rhs), None)
    start = (jnp.zeros((NWIN, WINDOW_PARAMS, WINDOW_PARAMS), jnp.float32), jnp.zeros((NWIN, WINDOW_PARAMS), jnp.float32))
    (matrix, rhs), _ = lax.scan(one_bundle, start, (local_slopes, global_slopes, residuals, weights, track_slot_count, windows))
    return (matrix, rhs)
```

```python
import jax
import jax.numpy as jnp
from jax import lax
from jax.experimental import pallas as pl
from jax.experimental.pallas import tpu as pltpu
from jax.sharding import Mesh
from jax.sharding import PartitionSpec as P

NWIN = 4
AXES = ("wide_0", "wide_1", "wide_2", "narrow_0", "narrow_1")
ALL = ("wide_0", "wide_1", "wide_2", "narrow_0", "narrow_1")
PLANE = ("wide_0", "narrow_1", "wide_2")
RING = ("wide_1", "narrow_0")
HI = lax.Precision.HIGHEST
F32 = jnp.float32


def tdot(left, right):
    return lax.dot_general(
        left, right, (((0,), (0,)), ((), ())), precision=HI, preferred_element_type=F32
    )


def iota(shape, dim):
    return lax.broadcasted_iota(jnp.int32, shape, dim)


def inverse(curv):
    size = 32
    lane, sub = iota((size, 128), 1), iota((size, 128), 0)
    rows = [curv[k * size : (k + 1) * size, :] for k in range(4)]
    for k in range(4):
        panel = rows[k]
        for t in range(size):
            at = k * size + t
            column = panel[:, at : at + 1]
            pivot = 1.0 / panel[t : t + 1, at : at + 1]
            fresh = jnp.where(lane[:1] == at, pivot, panel[t : t + 1, :] * pivot)
            panel = jnp.where(sub == t, fresh, jnp.where(lane == at, 0.0, panel) - column * fresh)
        others = [o for o in range(4) if o != k]
        rest = jnp.concatenate([rows[o] for o in others], axis=0)
        factor = rest[:, k * size : (k + 1) * size]
        inside = (iota((96, 128), 1) // size) == k
        rest = jnp.where(inside, 0.0, rest) - jnp.dot(
            factor, panel, precision=HI, preferred_element_type=F32
        )
        for n, o in enumerate(others):
            rows[o] = rest[n * size : (n + 1) * size, :]
        rows[k] = panel
    return jnp.concatenate(rows, axis=0)


def pick_lanes(pieces):
    place = iota(pieces[0].shape, 1) // 32
    out = pieces[3]
    for b in (2, 1, 0):
        out = jnp.where(place == b, pieces[b], out)
    return out


def roll32(value, by):
    by %= 4
    return value if by == 0 else pltpu.roll(value, by * 32, 1)


def assemble_kernel(count, window, weight, resid, local, glob, out, gp, vgp, matrix):
    live = jnp.where(iota((1, 512), 1) < count[0], weight[...], 0.0)
    vb = jnp.transpose(jnp.broadcast_to(live, (128, 512)))
    rb = jnp.transpose(jnp.broadcast_to(resid[...], (128, 512)))
    slopes = local[...]
    wl = slopes * vb
    curv = tdot(wl, slopes)
    curv = curv + jnp.where(iota((128, 128), 0) == iota((128, 128), 1), 1.0, 0.0)

    for x in range(4):
        for h in range(8):
            r = slice(h * 64, h * 64 + 64)
            first = glob[r, x * 256 : x * 256 + 128]
            second = glob[r, x * 256 + 128 : x * 256 + 256]
            even = pick_lanes([first, roll32(first, -1), roll32(second, 2), roll32(second, 1)])
            odd = pick_lanes([roll32(first, -1), roll32(first, 2), roll32(second, 1), second])
            gp[r, x * 128 : x * 128 + 128] = even
            gp[r, 512 + x * 128 : 512 + x * 128 + 128] = odd
            vgp[r, x * 128 : x * 128 + 128] = even * vb[r]
            vgp[r, 512 + x * 128 : 512 + x * 128 + 128] = odd * vb[r]

    coupling = tdot(wl, gp[...])
    lr = tdot(wl, rb)
    inv = inverse(curv)
    solved = jnp.dot(inv, coupling, precision=HI, preferred_element_type=F32)

    rhs = []
    for c in range(8):
        cols = slice(c * 128, c * 128 + 128)
        rhs.append(
            jnp.sum(vgp[:, cols] * rb, axis=0, keepdims=True)
            - jnp.sum(solved[:, cols] * lr, axis=0, keepdims=True)
        )

    for q in range(2):
        for jh in range(2):
            n = slice((q * 2 + jh) * 256, (q * 2 + jh) * 256 + 256)
            for p in range(2):
                for ih in range(2):
                    if (p == q and ih > jh) or (p != q and ih < jh):
                        continue
                    m = slice((p * 2 + ih) * 256, (p * 2 + ih) * 256 + 256)
                    matrix[m, n] = tdot(vgp[:, m], gp[:, n]) - tdot(solved[:, m], coupling[:, n])

    place = iota((32, 128), 1) // 32
    below = iota((32, 128), 0) >= iota((32, 128), 1) % 32
    ondiag = iota((32, 128), 0) == iota((32, 128), 1) % 32
    sub8 = iota((8, 128), 0)
    own = jnp.broadcast_to(window[0].astype(F32), (8, 128))
    for x in range(4):
        for y in range(4):
            extra = [pick_lanes([roll32(rhs[p * 4 + z], z - y) for z in range(4)]) for p in range(2)]
            i = x * 4 + y
            pair = matrix[512 + i * 32 : 512 + i * 32 + 32, x * 128 : x * 128 + 128]
            held = jnp.where(ondiag & (place == y), pair, 0.0)
            edge = roll32(jnp.sum(held, axis=0, keepdims=True), -y)
            tail = jnp.where(
                sub8 == 0,
                extra[0],
                jnp.where(sub8 == 1, extra[1], jnp.where(sub8 == 2, edge, own)),
            )
            for q in range(2):
                dest = (x * 4 + y) * 2 + q
                cols = slice(q * 512 + x * 128, q * 512 + x * 128 + 128)
                for z in range(4):
                    i = z * 4 + y
                    same = slice(q * 512 + i * 32, q * 512 + i * 32 + 32)
                    cross = slice((1 - q) * 512 + i * 32, (1 - q) * 512 + i * 32 + 32)
                    if i < x * 4:
                        tile = matrix[same, cols]
                    elif i > x * 4 + 3:
                        tile = matrix[cross, cols]
                    else:
                        j = place + x * 4
                        tile = jnp.where(
                            (j > i) | ((j == i) & below), matrix[same, cols], matrix[cross, cols]
                        )
                    out[dest, z * 32 : z * 32 + 32, :] = tile
                out[dest, 128:136, :] = tail


def windows_kernel(arrived, out):
    def sums(g):
        acc = [jnp.zeros((8, 128), F32) for _ in range(NWIN)]
        for s in range(32):
            block = arrived[s, pl.ds(g * 8, 8), :]
            which = jnp.broadcast_to(arrived[s, 131:132, :], (8, 128))
            for w in range(NWIN):
                acc[w] = acc[w] + jnp.where(which == float(w), block, 0.0)
        return acc

    @pl.loop(0, 4)
    def _(z):
        for k in range(4):
            acc = sums(z * 4 + k)
            for b in range(4):
                out[b * 4 + z, k * 8 : k * 8 + 8, :] = pick_lanes(
                    [roll32(acc[w], w - b) for w in range(NWIN)]
                )

    acc = sums(16)
    packed = [pick_lanes([roll32(acc[w], w - b) for w in range(NWIN)]) for b in range(4)]
    for z in range(4):
        tail = jnp.where(iota((8, 128), 0) == 2, packed[0], packed[z])
        for b in range(4):
            out[b * 4 + z, 32:40, :] = tail


def ring_kernel(arrived, out):
    total = arrived[0]
    for s in range(1, 16):
        total = total + arrived[s]
    out[...] = total


def finish_kernel(mine, other, out, rhs):
    x, zh, q = lax.axis_index("wide_0"), lax.axis_index("wide_1"), lax.axis_index("wide_2")
    zl, y = lax.axis_index("narrow_0"), lax.axis_index("narrow_1")
    i, j = zl * 4 + y, x * 4 + zh
    diag = jnp.broadcast_to(i == j, (32, 32))
    half = jnp.where(i <= j, q, 1 - q)
    lower = jnp.broadcast_to(half == 0, (32, 32))
    a, b = iota((32, 32), 0), iota((32, 32), 1)
    turned = jnp.transpose(mine[0:32, :])
    for w in range(NWIN):
        cols = slice(w * 32, w * 32 + 32)
        held, theirs = mine[0:32, cols], other[0:32, cols]
        flip = turned[cols, :]
        edge = jnp.broadcast_to(mine[34:35, cols], (32, 32))
        own_part = jnp.where(diag & (a >= b), held, flip)
        other_part = jnp.where(diag & (a == b), edge, jnp.where(diag & (a > b), flip, theirs))
        out[w, :, 0:32] = jnp.where(lower, own_part, other_part)
        out[w, :, 32:64] = jnp.where(lower, other_part, own_part)
        rhs[w : w + 1, 0:32] = mine[32:33, cols]
        rhs[w : w + 1, 32:64] = mine[33:34, cols]


def vmem(count):
    return [pl.BlockSpec(memory_space=pltpu.VMEM)] * count


def turn_pairs():
    place = lambda x, zh, q, zl, y: (((x * 4 + zh) * 2 + q) * 4 + zl) * 4 + y
    pairs = []
    for x in range(4):
        for zh in range(4):
            for q in range(2):
                for zl in range(4):
                    for y in range(4):
                        i, j = zl * 4 + y, x * 4 + zh
                        p = q if i <= j else 1 - q
                        target = 1 - q if i == j else p
                        pairs.append((place(x, zh, q, zl, y), place(zl, y, target, x, zh)))
    return pairs


def on_device(local_slopes, global_slopes, residuals, weights, track_slot_count, windows):
    big = pltpu.CompilerParams(vmem_limit_bytes=48 << 20)
    payload = pl.pallas_call(
        assemble_kernel,
        out_shape=jax.ShapeDtypeStruct((32, 136, 128), F32),
        in_specs=[pl.BlockSpec(memory_space=pltpu.SMEM)] * 2 + vmem(4),
        out_specs=vmem(1)[0],
        scratch_shapes=[
            pltpu.VMEM((512, 1024), F32),
            pltpu.VMEM((512, 1024), F32),
            pltpu.VMEM((1024, 1024), F32),
        ],
        compiler_params=big,
        name="assemble",
    )(track_slot_count, windows, weights, residuals, local_slopes[0], global_slopes[0])
    arrived = lax.all_to_all(payload, PLANE, split_axis=0, concat_axis=0, tiled=True)
    packed = pl.pallas_call(
        windows_kernel,
        out_shape=jax.ShapeDtypeStruct((16, 40, 128), F32),
        in_specs=vmem(1),
        out_specs=vmem(1)[0],
        compiler_params=big,
        name="window_sums",
    )(arrived)
    ring = lax.all_to_all(packed, RING, split_axis=0, concat_axis=0, tiled=True)
    mine = pl.pallas_call(
        ring_kernel,
        out_shape=jax.ShapeDtypeStruct((40, 128), F32),
        in_specs=vmem(1),
        out_specs=vmem(1)[0],
        name="ring_sums",
    )(ring)
    other = lax.ppermute(mine, ALL, turn_pairs())
    out, rhs = pl.pallas_call(
        finish_kernel,
        out_shape=(
            jax.ShapeDtypeStruct((NWIN, 32, 64), F32),
            jax.ShapeDtypeStruct((NWIN, 64), F32),
        ),
        in_specs=vmem(2),
        out_specs=tuple(vmem(2)),
        name="finish",
    )(mine, other)
    return jnp.transpose(out, (0, 2, 1)), rhs


def solution(mesh):
    split = Mesh(mesh.devices.reshape(4, 4, 2, 4, 4), AXES)
    return jax.shard_map(
        on_device,
        mesh=split,
        in_specs=(
            P(AXES, None, None),
            P(AXES, None, None),
            P(AXES, None),
            P(AXES, None),
            P(AXES),
            P(AXES),
        ),
        out_specs=(
            P(None, ("narrow_0", "narrow_1"), ("wide_0", "wide_1", "wide_2")),
            P(None, ("narrow_0", "narrow_1")),
        ),
        check_vma=False,
    )
```

```python
import functools

import jax
import jax.numpy as jnp
from jax import lax
from jax.experimental import pallas as pl
from jax.experimental.pallas import tpu as pltpu
from jax.sharding import Mesh
from jax.sharding import PartitionSpec as P

NWIN = 4
AXES = ("wide_0", "wide_1", "wide_2", "narrow_0", "narrow_1", "narrow_2")
NARROW = AXES[3:]
WIDE = AXES[:3]
PLANE = ("wide_0", "narrow_2", "wide_2", "narrow_1")
RING = ("wide_1", "narrow_0")
HI = lax.Precision.HIGHEST
F32 = jnp.float32
BF16 = jnp.bfloat16


def iota(shape, dim):
    return lax.broadcasted_iota(jnp.int32, shape, dim)


def total_of(parts):
    while len(parts) > 1:
        parts = [a + b for a, b in zip(parts[::2], parts[1::2])] + parts[len(parts) & ~1 :]
    return parts[0]


def sweep(curv, chores):
    full = (8, 128)
    lane, sub = iota(full, 1), iota(full, 0)
    rows = [curv[8 * k : 8 * k + 8, :] for k in range(16)]
    for k in range(16):
        panel = rows[k]
        cols = [jnp.broadcast_to(panel[:, 8 * k + j : 8 * k + j + 1], full) for j in range(8)]
        held = {}
        for j in range(8):
            for i in range(j + 1):
                held[i, j] = jnp.broadcast_to(cols[j][i : i + 1, :], full)

        def at(i, j):
            return held[min(i, j), max(i, j)]

        for t in range(0, 8, 2):
            a, b, d = at(t, t), at(t, t + 1), at(t + 1, t + 1)
            det = 1.0 / (a * d - b * b)
            rest = [i for i in range(8) if i not in (t, t + 1)]
            one = {i: at(i, t) for i in rest}
            two = {i: at(i, t + 1) for i in rest}
            new_one = {i: (d * one[i] - b * two[i]) * det for i in rest}
            new_two = {i: (a * two[i] - b * one[i]) * det for i in rest}
            for j in rest:
                for i in rest:
                    if i <= j:
                        held[i, j] = held[i, j] - (one[i] * new_one[j] + two[i] * new_two[j])
            for i in rest:
                held[min(i, t), max(i, t)] = new_one[i]
                held[min(i, t + 1), max(i, t + 1)] = new_two[i]
            held[t, t], held[t, t + 1], held[t + 1, t + 1] = -d * det, b * det, -a * det
        columns = []
        for u in range(8):
            layer = [at(i, u) for i in range(8)]
            for bit in (1, 2, 4):
                layer = [
                    jnp.where((sub & bit) == 0, low, high) for low, high in zip(layer[::2], layer[1::2])
                ]
            columns.append(layer[0])
        inside = (lane // 8) == k
        panel = jnp.where(inside, jnp.where(lane % 8 == sub, 1.0, 0.0), panel)
        panel = -total_of([columns[u] * panel[u : u + 1, :] for u in range(8)])
        spread = [jnp.broadcast_to(panel[u : u + 1, :], full) for u in range(8)]
        for o in list(range(k + 1, 16)) + list(range(k)):
            was = rows[o]
            parts = [
                jnp.broadcast_to(was[:, 8 * k + u : 8 * k + u + 1], full) * spread[u] for u in range(8)
            ]
            rows[o] = jnp.where(inside, 0.0, was) - total_of(parts)
        rows[k] = panel
        for chore in chores[k]:
            chore()
    return jnp.concatenate(rows, axis=0)


def pick_lanes(pieces):
    place = iota(pieces[0].shape, 1) // 32
    out = pieces[3]
    for b in (2, 1, 0):
        out = jnp.where(place == b, pieces[b], out)
    return out


def roll32(value, by):
    by %= 4
    return value if by == 0 else pltpu.roll(value, by * 32, 1)


def dot(left, right, precision=HI):
    return jnp.dot(left, right, precision=precision, preferred_element_type=F32)


def halves(value):
    high = value.astype(BF16)
    return high, (value - high.astype(F32)).astype(BF16)


def assemble_kernel(count, window, weight, resid, local, glob, out, *scratch):
    wv, rv, lv, gv, gp, up, gh, gl, matrix, sems = scratch
    copies = [
        pltpu.make_async_copy(source, target, sems.at[n])
        for n, (source, target) in enumerate(((local, lv), (weight, wv), (resid, rv), (glob, gv)))
    ]
    for copy in copies:
        copy.start()
    for copy in copies[:3]:
        copy.wait()
    live = jnp.where(iota((1, 512), 1) < count[0], wv[...], 0.0)
    vb = jnp.transpose(jnp.broadcast_to(live, (128, 512)))
    rb = jnp.transpose(jnp.broadcast_to(rv[...], (128, 512)))
    slopes = lv[...]
    wlt = jnp.transpose(slopes) * live
    curv = dot(wlt, slopes)
    curv = curv + jnp.where(iota((128, 128), 0) == iota((128, 128), 1), 1.0, 0.0)
    copies[3].wait()

    def permute(h):
        r = slice(h * 32, h * 32 + 32)
        for x in range(4):
            first = gv[r, x * 256 : x * 256 + 128]
            second = gv[r, x * 256 + 128 : x * 256 + 256]
            gp[r, x * 128 : x * 128 + 128] = pick_lanes(
                [first, roll32(first, -1), roll32(second, 2), roll32(second, 1)]
            )
            gp[r, 512 + x * 128 : 512 + x * 128 + 128] = pick_lanes(
                [roll32(first, -1), roll32(first, 2), roll32(second, 1), second]
            )

    def turn(k, c):
        cols, r = slice(c * 128, c * 128 + 128), slice(k * 128, k * 128 + 128)
        gh[cols, r], gl[cols, r] = halves(jnp.transpose(gp[r, cols]))

    def couple(c):
        cols = slice(c * 128, c * 128 + 128)
        up[:, cols] = dot(wlt, gp[:, cols])

    chores = [[] for _ in range(16)]
    for h in range(16):
        chores[h // 2].append(functools.partial(permute, h))
    for c in range(8):
        chores[8 + c].append(functools.partial(couple, c))
        for k in range(4):
            chores[8 + c].append(functools.partial(turn, k, c))
    inv = sweep(curv, chores)

    rhs = []
    for q in range(2):
        for jh in range(2):
            n = slice((q * 2 + jh) * 256, (q * 2 + jh) * 256 + 256)
            left = gp[:, n] - dot(slopes, dot(inv, up[:, n]))
            parts = [left[:, :128] * vb, left[:, 128:] * vb]
            rhs += [jnp.sum(part * rb, axis=0, keepdims=True) for part in parts]
            zh, zl = halves(jnp.concatenate(parts, axis=1))
            for p in range(2):
                for ih in range(2):
                    if (p == q and ih > jh) or (p != q and ih < jh):
                        continue
                    m = slice((p * 2 + ih) * 256, (p * 2 + ih) * 256 + 256)
                    matrix[m, n] = dot(gh[m, :], zh, None) + dot(gh[m, :], zl, None) + dot(gl[m, :], zh, None)

    place = iota((32, 128), 1) // 32
    below = iota((32, 128), 0) >= iota((32, 128), 1) % 32
    ondiag = iota((32, 128), 0) == iota((32, 128), 1) % 32
    sub8 = iota((8, 128), 0)
    own = jnp.broadcast_to(window[0].astype(F32), (8, 128))
    for x in range(4):
        for y in range(4):
            i = x * 4 + y
            pair = matrix[512 + i * 32 : 512 + i * 32 + 32, x * 128 : x * 128 + 128]
            held = jnp.where(ondiag & (place == y), pair, 0.0)
            edge = roll32(jnp.sum(held, axis=0, keepdims=True), -y)
            tails = []
            for b in range(2):
                sums = pick_lanes(
                    [
                        roll32(rhs[p * 4 + a * 2 + b], p * 2 + a - y)
                        for p in range(2)
                        for a in range(2)
                    ]
                )
                tails.append(jnp.where(sub8 == 0, sums, jnp.where(sub8 == 1, edge, own)))
            for q in range(2):
                dest = ((x * 4 + y) * 2 + q) * 2
                cols = slice(q * 512 + x * 128, q * 512 + x * 128 + 128)
                for z in range(4):
                    i = z * 4 + y
                    same = slice(q * 512 + i * 32, q * 512 + i * 32 + 32)
                    cross = slice((1 - q) * 512 + i * 32, (1 - q) * 512 + i * 32 + 32)
                    if i < x * 4:
                        tile = matrix[same, cols]
                    elif i > x * 4 + 3:
                        tile = matrix[cross, cols]
                    else:
                        j = place + x * 4
                        tile = jnp.where(
                            (j > i) | ((j == i) & below), matrix[same, cols], matrix[cross, cols]
                        )
                    out[dest + z % 2, z // 2 * 32 : z // 2 * 32 + 32, :] = tile
                for b in range(2):
                    out[dest + b, 64:72, :] = tails[b]


def windows_kernel(arrived, out):
    def sums(g):
        acc = [jnp.zeros((8, 128), F32) for _ in range(NWIN)]
        for s in range(64):
            block = arrived[s, pl.ds(g * 8, 8), :]
            which = jnp.broadcast_to(arrived[s, 66:67, :], (8, 128))
            for w in range(NWIN):
                acc[w] = acc[w] + jnp.where(which == float(w), block, 0.0)
        return acc

    def packed(acc, back):
        return pick_lanes([roll32(acc[w], w - back) for w in range(NWIN)])

    @pl.loop(0, 2)
    def _(a):
        for k in range(4):
            acc = sums(a * 4 + k)
            for h in range(4):
                out[h * 2 + a, k * 8 : k * 8 + 8, :] = packed(acc, h)

    acc = sums(8)
    sub = iota((8, 128), 0)
    edge = jnp.broadcast_to(packed(acc, 0)[1:2, :], (8, 128))
    for a in range(2):
        first = jnp.broadcast_to(packed(acc, a)[0:1, :], (8, 128))
        second = jnp.broadcast_to(packed(acc, 2 + a)[0:1, :], (8, 128))
        tail = jnp.where(sub == 0, first, jnp.where(sub == 1, second, edge))
        for h in range(4):
            out[h * 2 + a, 32:40, :] = tail


def ring_kernel(arrived, out):
    total = arrived[0]
    for s in range(1, 8):
        total = total + arrived[s]
    out[...] = total


def finish_kernel(mine, other, out, rhs):
    x, zh, q = lax.axis_index("wide_0"), lax.axis_index("wide_1"), lax.axis_index("wide_2")
    zl = lax.axis_index("narrow_0") * 2 + lax.axis_index("narrow_1")
    y = lax.axis_index("narrow_2")
    i, j = zl * 4 + y, x * 4 + zh
    diag = jnp.broadcast_to(i == j, (32, 32))
    half = jnp.where(i <= j, q, 1 - q)
    lower = jnp.broadcast_to(half == 0, (32, 32))
    a, b = iota((32, 32), 0), iota((32, 32), 1)
    turned = jnp.transpose(mine[0:32, :])
    for w in range(NWIN):
        cols = slice(w * 32, w * 32 + 32)
        held, theirs = mine[0:32, cols], other[0:32, cols]
        flip = turned[cols, :]
        edge = jnp.broadcast_to(mine[34:35, cols], (32, 32))
        own_part = jnp.where(diag & (a >= b), held, flip)
        other_part = jnp.where(diag & (a == b), edge, jnp.where(diag & (a > b), flip, theirs))
        out[w, :, 0:32] = jnp.where(lower, own_part, other_part)
        out[w, :, 32:64] = jnp.where(lower, other_part, own_part)
        rhs[w : w + 1, 0:32] = mine[32:33, cols]
        rhs[w : w + 1, 32:64] = mine[33:34, cols]


def vmem(count):
    return [pl.BlockSpec(memory_space=pltpu.VMEM)] * count


def turn_pairs():
    place = lambda x, zh, q, zl, y: (((x * 4 + zh) * 2 + q) * 4 + zl) * 4 + y
    pairs = []
    for x in range(4):
        for zh in range(4):
            for q in range(2):
                for zl in range(4):
                    for y in range(4):
                        i, j = zl * 4 + y, x * 4 + zh
                        p = q if i <= j else 1 - q
                        target = 1 - q if i == j else p
                        pairs.append((place(x, zh, q, zl, y), place(zl, y, target, x, zh)))
    return pairs


def on_device(local_slopes, global_slopes, residuals, weights, track_slot_count, windows):
    small = pltpu.CompilerParams(vmem_limit_bytes=8 << 20)
    big = pltpu.CompilerParams(vmem_limit_bytes=48 << 20)
    payload = pl.pallas_call(
        assemble_kernel,
        out_shape=jax.ShapeDtypeStruct((64, 72, 128), F32),
        in_specs=[pl.BlockSpec(memory_space=pltpu.SMEM)] * 2 + [pl.BlockSpec(memory_space=pltpu.HBM)] * 4,
        out_specs=vmem(1)[0],
        scratch_shapes=[
            pltpu.VMEM((1, 512), F32),
            pltpu.VMEM((1, 512), F32),
            pltpu.VMEM((512, 128), F32),
            pltpu.VMEM((512, 1024), F32),
            pltpu.VMEM((512, 1024), F32),
            pltpu.VMEM((128, 1024), F32),
            pltpu.VMEM((1024, 512), BF16),
            pltpu.VMEM((1024, 512), BF16),
            pltpu.VMEM((1024, 1024), F32),
            pltpu.SemaphoreType.DMA((4,)),
        ],
        compiler_params=big,
        name="assemble",
    )(
        track_slot_count,
        windows,
        *[
            pltpu.with_memory_space_constraint(value, pltpu.HBM)
            for value in (weights, residuals, local_slopes[0], global_slopes[0])
        ],
    )
    arrived = lax.all_to_all(payload, PLANE, split_axis=0, concat_axis=0, tiled=True)
    packed = pl.pallas_call(
        windows_kernel,
        out_shape=jax.ShapeDtypeStruct((8, 40, 128), F32),
        in_specs=vmem(1),
        out_specs=vmem(1)[0],
        compiler_params=big,
        name="window_sums",
    )(arrived)
    ring = lax.all_to_all(packed, RING, split_axis=0, concat_axis=0, tiled=True)
    mine = pl.pallas_call(
        ring_kernel,
        out_shape=jax.ShapeDtypeStruct((40, 128), F32),
        in_specs=vmem(1),
        out_specs=vmem(1)[0],
        compiler_params=small,
        name="ring_sums",
    )(ring)
    other = lax.ppermute(mine, AXES, turn_pairs())
    out, rhs = pl.pallas_call(
        finish_kernel,
        out_shape=(
            jax.ShapeDtypeStruct((NWIN, 32, 64), F32),
            jax.ShapeDtypeStruct((NWIN, 64), F32),
        ),
        in_specs=vmem(2),
        out_specs=tuple(vmem(2)),
        compiler_params=small,
        name="finish",
    )(mine, other)
    return jnp.transpose(out, (0, 2, 1)), rhs


def solution(mesh):
    split = Mesh(mesh.devices.reshape(4, 4, 2, 2, 2, 4), AXES)
    return jax.shard_map(
        on_device,
        mesh=split,
        in_specs=(
            P(AXES, None, None),
            P(AXES, None, None),
            P(AXES, None),
            P(AXES, None),
            P(AXES),
            P(AXES),
        ),
        out_specs=(
            P(None, NARROW, WIDE),
            P(None, NARROW),
        ),
        check_vma=False,
    )
```

```python
import functools

import jax
import jax.numpy as jnp
from jax import lax
from jax.experimental import pallas as pl
from jax.experimental.pallas import tpu as pltpu
from jax.sharding import Mesh
from jax.sharding import PartitionSpec as P

NWIN = 4
AXES = ("wide_0", "wide_1", "wide_2", "narrow_0", "narrow_1", "narrow_2")
NARROW = AXES[3:]
WIDE = AXES[:3]
PLANE = ("wide_0", "narrow_2", "wide_2", "narrow_1")
RING = ("wide_1", "narrow_0")
HI = lax.Precision.HIGHEST
F32 = jnp.float32
BF16 = jnp.bfloat16


def iota(shape, dim):
    return lax.broadcasted_iota(jnp.int32, shape, dim)


def total_of(parts):
    while len(parts) > 1:
        parts = [a + b for a, b in zip(parts[::2], parts[1::2])] + parts[len(parts) & ~1 :]
    return parts[0]


def factor(curv, chores):
    full = (8, 128)
    lane, sub = iota(full, 1), iota(full, 0)
    rows = [curv[8 * k : 8 * k + 8, :] for k in range(16)]
    lower, scaled = [], []
    for k in range(16):
        panel = rows[k]
        cols = [jnp.broadcast_to(panel[:, 8 * k + j : 8 * k + j + 1], full) for j in range(8)]
        held = {}
        for j in range(8):
            for i in range(j + 1):
                held[i, j] = jnp.broadcast_to(cols[j][i : i + 1, :], full)

        def at(i, j):
            return held[min(i, j), max(i, j)]

        for t in range(0, 8, 2):
            a, b, d = at(t, t), at(t, t + 1), at(t + 1, t + 1)
            det = 1.0 / (a * d - b * b)
            rest = [i for i in range(8) if i not in (t, t + 1)]
            one = {i: at(i, t) for i in rest}
            two = {i: at(i, t + 1) for i in rest}
            new_one = {i: (d * one[i] - b * two[i]) * det for i in rest}
            new_two = {i: (a * two[i] - b * one[i]) * det for i in rest}
            for j in rest:
                for i in rest:
                    if i <= j:
                        held[i, j] = held[i, j] - (one[i] * new_one[j] + two[i] * new_two[j])
            for i in rest:
                held[min(i, t), max(i, t)] = new_one[i]
                held[min(i, t + 1), max(i, t + 1)] = new_two[i]
            held[t, t], held[t, t + 1], held[t + 1, t + 1] = -d * det, b * det, -a * det
        columns = []
        for u in range(8):
            layer = [at(i, u) for i in range(8)]
            for bit in (1, 2, 4):
                layer = [
                    jnp.where((sub & bit) == 0, low, high) for low, high in zip(layer[::2], layer[1::2])
                ]
            columns.append(layer[0])
        inside = (lane // 8) == k
        panel = jnp.where(inside, jnp.where(lane % 8 == sub, 1.0, 0.0), panel)
        lower.append(jnp.where(lane < 8 * k + 8, panel, 0.0))
        panel = -total_of([columns[u] * panel[u : u + 1, :] for u in range(8)])
        spread = [jnp.broadcast_to(panel[u : u + 1, :], full) for u in range(8)]
        for o in range(k + 1, 16):
            was = rows[o]
            parts = [
                jnp.broadcast_to(was[:, 8 * k + u : 8 * k + u + 1], full) * spread[u] for u in range(8)
            ]
            rows[o] = jnp.where(inside, 0.0, was) - total_of(parts)
        scaled.append(jnp.where(lane < 8 * k + 8, panel, 0.0))
        for chore in chores[k]:
            chore()
    return jnp.concatenate(lower, axis=0), jnp.concatenate(scaled, axis=0)


def pick_lanes(pieces):
    place = iota(pieces[0].shape, 1) // 32
    out = pieces[3]
    for b in (2, 1, 0):
        out = jnp.where(place == b, pieces[b], out)
    return out


def roll32(value, by):
    by %= 4
    return value if by == 0 else pltpu.roll(value, by * 32, 1)


def dot(left, right, precision=HI):
    return jnp.dot(left, right, precision=precision, preferred_element_type=F32)


def halves(value):
    high = value.astype(BF16)
    return high, (value - high.astype(F32)).astype(BF16)


def assemble_kernel(count, window, weight, resid, local, glob, out, *scratch):
    wv, rv, lv, gv, gp, right, turned, middle, stack, matrix, sems = scratch
    copies = [
        pltpu.make_async_copy(source, target, sems.at[n])
        for n, (source, target) in enumerate(((local, lv), (weight, wv), (resid, rv), (glob, gv)))
    ]
    for copy in copies:
        copy.start()
    for copy in copies[:3]:
        copy.wait()
    live = jnp.where(iota((1, 512), 1) < count[0], wv[...], 0.0)
    rb = jnp.transpose(jnp.broadcast_to(rv[...], (128, 512)))
    slopes = lv[...]
    wlt = jnp.transpose(slopes) * live
    curv = dot(wlt, slopes)
    curv = curv + jnp.where(iota((128, 128), 0) == iota((128, 128), 1), 1.0, 0.0)
    copies[3].wait()

    def permute(h):
        r = slice(h * 32, h * 32 + 32)
        for x in range(4):
            first = gv[r, x * 256 : x * 256 + 128]
            second = gv[r, x * 256 + 128 : x * 256 + 256]
            even = pick_lanes([first, roll32(first, -1), roll32(second, 2), roll32(second, 1)])
            odd = pick_lanes([roll32(first, -1), roll32(first, 2), roll32(second, 1), second])
            for value, start in ((even, x * 128), (odd, 512 + x * 128)):
                cols = slice(start, start + 128)
                gp[r, cols] = value
                high, low = halves(value)
                right[h * 32 : h * 32 + 32, cols] = high
                right[512 + h * 32 : 512 + h * 32 + 32, cols] = low
                right[1024 + h * 32 : 1024 + h * 32 + 32, cols] = high

    def turn(k, c):
        cols = slice(c * 128, c * 128 + 128)
        high, low = halves(jnp.transpose(gp[k * 128 : k * 128 + 128, cols]))
        for place, value in enumerate((high, high, low)):
            turned[cols, place * 512 + k * 128 : place * 512 + k * 128 + 128] = value

    chores = [[] for _ in range(16)]
    for h in range(16):
        chores[h // 2].append(functools.partial(permute, h))
    for c in range(8):
        for k in range(4):
            chores[8 + c].append(functools.partial(turn, k, c))
    wl = jnp.transpose(wlt)
    lower, scaled = factor(curv, chores)

    solved = dot(scaled, wlt)
    forward = lax.dot_general(
        wl, lower, (((1,), (1,)), ((), ())), precision=HI, preferred_element_type=F32
    )
    for k in range(4):
        r = slice(k * 128, k * 128 + 128)
        same = iota((128, 512), 0) + k * 128 == iota((128, 512), 1)
        high, low = halves(jnp.where(same, live, 0.0) - dot(forward[r], solved))
        for place, value in enumerate((high, high, low)):
            middle[r, place * 512 : place * 512 + 512] = value

    for c in range(4):
        cols = slice(c * 256, c * 256 + 256)
        gv[:, cols] = dot(middle[...], right[:, cols], None)
    rhs = []
    for c in range(8):
        cols = slice(c * 128, c * 128 + 128)
        left = gv[:, cols]
        rhs.append(jnp.sum(left * rb, axis=0, keepdims=True))
        high, low = halves(left)
        for place, value in enumerate((high, low, high)):
            stack[place * 512 : place * 512 + 512, cols] = value

    for q in range(2):
        for jh in range(2):
            n = slice((q * 2 + jh) * 256, (q * 2 + jh) * 256 + 256)
            for p in range(2):
                for ih in range(2):
                    if (p == q and ih > jh) or (p != q and ih < jh):
                        continue
                    m = slice((p * 2 + ih) * 256, (p * 2 + ih) * 256 + 256)
                    matrix[m, n] = dot(turned[m, :], stack[:, n], None)

    place = iota((32, 128), 1) // 32
    below = iota((32, 128), 0) >= iota((32, 128), 1) % 32
    ondiag = iota((32, 128), 0) == iota((32, 128), 1) % 32
    sub8 = iota((8, 128), 0)
    own = jnp.broadcast_to(window[0].astype(F32), (8, 128))
    for x in range(4):
        for y in range(4):
            i = x * 4 + y
            pair = matrix[512 + i * 32 : 512 + i * 32 + 32, x * 128 : x * 128 + 128]
            held = jnp.where(ondiag & (place == y), pair, 0.0)
            edge = roll32(jnp.sum(held, axis=0, keepdims=True), -y)
            tails = []
            for b in range(2):
                sums = pick_lanes(
                    [
                        roll32(rhs[p * 4 + a * 2 + b], p * 2 + a - y)
                        for p in range(2)
                        for a in range(2)
                    ]
                )
                tails.append(jnp.where(sub8 == 0, sums, jnp.where(sub8 == 1, edge, own)))
            for q in range(2):
                dest = ((x * 4 + y) * 2 + q) * 2
                cols = slice(q * 512 + x * 128, q * 512 + x * 128 + 128)
                for z in range(4):
                    i = z * 4 + y
                    same = slice(q * 512 + i * 32, q * 512 + i * 32 + 32)
                    cross = slice((1 - q) * 512 + i * 32, (1 - q) * 512 + i * 32 + 32)
                    if i < x * 4:
                        tile = matrix[same, cols]
                    elif i > x * 4 + 3:
                        tile = matrix[cross, cols]
                    else:
                        j = place + x * 4
                        tile = jnp.where(
                            (j > i) | ((j == i) & below), matrix[same, cols], matrix[cross, cols]
                        )
                    out[dest + z % 2, z // 2 * 32 : z // 2 * 32 + 32, :] = tile
                for b in range(2):
                    out[dest + b, 64:72, :] = tails[b]


def windows_kernel(arrived, out):
    def sums(g):
        acc = [jnp.zeros((8, 128), F32) for _ in range(NWIN)]
        for s in range(64):
            block = arrived[s, pl.ds(g * 8, 8), :]
            which = jnp.broadcast_to(arrived[s, 66:67, :], (8, 128))
            for w in range(NWIN):
                acc[w] = acc[w] + jnp.where(which == float(w), block, 0.0)
        return acc

    def packed(acc, back):
        return pick_lanes([roll32(acc[w], w - back) for w in range(NWIN)])

    @pl.loop(0, 2)
    def _(a):
        for k in range(4):
            acc = sums(a * 4 + k)
            for h in range(4):
                out[h * 2 + a, k * 8 : k * 8 + 8, :] = packed(acc, h)

    acc = sums(8)
    sub = iota((8, 128), 0)
    edge = jnp.broadcast_to(packed(acc, 0)[1:2, :], (8, 128))
    for a in range(2):
        first = jnp.broadcast_to(packed(acc, a)[0:1, :], (8, 128))
        second = jnp.broadcast_to(packed(acc, 2 + a)[0:1, :], (8, 128))
        tail = jnp.where(sub == 0, first, jnp.where(sub == 1, second, edge))
        for h in range(4):
            out[h * 2 + a, 32:40, :] = tail


def ring_kernel(arrived, out):
    total = arrived[0]
    for s in range(1, 8):
        total = total + arrived[s]
    out[...] = total


def finish_kernel(mine, other, out, rhs):
    x, zh, q = lax.axis_index("wide_0"), lax.axis_index("wide_1"), lax.axis_index("wide_2")
    zl = lax.axis_index("narrow_0") * 2 + lax.axis_index("narrow_1")
    y = lax.axis_index("narrow_2")
    i, j = zl * 4 + y, x * 4 + zh
    diag = jnp.broadcast_to(i == j, (32, 32))
    half = jnp.where(i <= j, q, 1 - q)
    lower = jnp.broadcast_to(half == 0, (32, 32))
    a, b = iota((32, 32), 0), iota((32, 32), 1)
    turned = jnp.transpose(mine[0:32, :])
    for w in range(NWIN):
        cols = slice(w * 32, w * 32 + 32)
        held, theirs = mine[0:32, cols], other[0:32, cols]
        flip = turned[cols, :]
        edge = jnp.broadcast_to(mine[34:35, cols], (32, 32))
        own_part = jnp.where(diag & (a >= b), held, flip)
        other_part = jnp.where(diag & (a == b), edge, jnp.where(diag & (a > b), flip, theirs))
        out[w, :, 0:32] = jnp.where(lower, own_part, other_part)
        out[w, :, 32:64] = jnp.where(lower, other_part, own_part)
        rhs[w : w + 1, 0:32] = mine[32:33, cols]
        rhs[w : w + 1, 32:64] = mine[33:34, cols]


def vmem(count):
    return [pl.BlockSpec(memory_space=pltpu.VMEM)] * count


def turn_pairs():
    place = lambda x, zh, q, zl, y: (((x * 4 + zh) * 2 + q) * 4 + zl) * 4 + y
    pairs = []
    for x in range(4):
        for zh in range(4):
            for q in range(2):
                for zl in range(4):
                    for y in range(4):
                        i, j = zl * 4 + y, x * 4 + zh
                        p = q if i <= j else 1 - q
                        target = 1 - q if i == j else p
                        pairs.append((place(x, zh, q, zl, y), place(zl, y, target, x, zh)))
    return pairs


def on_device(local_slopes, global_slopes, residuals, weights, track_slot_count, windows):
    small = pltpu.CompilerParams(vmem_limit_bytes=8 << 20)
    big = pltpu.CompilerParams(vmem_limit_bytes=48 << 20)
    payload = pl.pallas_call(
        assemble_kernel,
        out_shape=jax.ShapeDtypeStruct((64, 72, 128), F32),
        in_specs=[pl.BlockSpec(memory_space=pltpu.SMEM)] * 2 + [pl.BlockSpec(memory_space=pltpu.HBM)] * 4,
        out_specs=vmem(1)[0],
        scratch_shapes=[
            pltpu.VMEM((1, 512), F32),
            pltpu.VMEM((1, 512), F32),
            pltpu.VMEM((512, 128), F32),
            pltpu.VMEM((512, 1024), F32),
            pltpu.VMEM((512, 1024), F32),
            pltpu.VMEM((1536, 1024), BF16),
            pltpu.VMEM((1024, 1536), BF16),
            pltpu.VMEM((512, 1536), BF16),
            pltpu.VMEM((1536, 1024), BF16),
            pltpu.VMEM((1024, 1024), F32),
            pltpu.SemaphoreType.DMA((4,)),
        ],
        compiler_params=big,
        name="assemble",
    )(
        track_slot_count,
        windows,
        *[
            pltpu.with_memory_space_constraint(value, pltpu.HBM)
            for value in (weights, residuals, local_slopes[0], global_slopes[0])
        ],
    )
    arrived = lax.all_to_all(payload, PLANE, split_axis=0, concat_axis=0, tiled=True)
    packed = pl.pallas_call(
        windows_kernel,
        out_shape=jax.ShapeDtypeStruct((8, 40, 128), F32),
        in_specs=vmem(1),
        out_specs=vmem(1)[0],
        compiler_params=big,
        name="window_sums",
    )(arrived)
    ring = lax.all_to_all(packed, RING, split_axis=0, concat_axis=0, tiled=True)
    mine = pl.pallas_call(
        ring_kernel,
        out_shape=jax.ShapeDtypeStruct((40, 128), F32),
        in_specs=vmem(1),
        out_specs=vmem(1)[0],
        compiler_params=small,
        name="ring_sums",
    )(ring)
    other = lax.ppermute(mine, AXES, turn_pairs())
    out, rhs = pl.pallas_call(
        finish_kernel,
        out_shape=(
            jax.ShapeDtypeStruct((NWIN, 32, 64), F32),
            jax.ShapeDtypeStruct((NWIN, 64), F32),
        ),
        in_specs=vmem(2),
        out_specs=tuple(vmem(2)),
        compiler_params=small,
        name="finish",
    )(mine, other)
    return jnp.transpose(out, (0, 2, 1)), rhs


def solution(mesh):
    split = Mesh(mesh.devices.reshape(4, 4, 2, 2, 2, 4), AXES)
    return jax.shard_map(
        on_device,
        mesh=split,
        in_specs=(
            P(AXES, None, None),
            P(AXES, None, None),
            P(AXES, None),
            P(AXES, None),
            P(AXES),
            P(AXES),
        ),
        out_specs=(
            P(None, NARROW, WIDE),
            P(None, NARROW),
        ),
        check_vma=False,
    )
```

```python
import functools

import jax
import jax.numpy as jnp
from jax import lax
from jax.experimental import pallas as pl
from jax.experimental.pallas import tpu as pltpu
from jax.sharding import Mesh
from jax.sharding import PartitionSpec as P

NWIN = 4
AXES = ("wide_0", "wide_1", "wide_2", "narrow_0", "narrow_1", "narrow_2")
NARROW = AXES[3:]
WIDE = AXES[:3]
PLANE = ("wide_0", "narrow_2", "wide_2", "narrow_1")
RING = ("wide_1", "narrow_0")
HI = lax.Precision.HIGHEST
F32 = jnp.float32
BF16 = jnp.bfloat16


def iota(shape, dim):
    return lax.broadcasted_iota(jnp.int32, shape, dim)


def total_of(parts):
    while len(parts) > 1:
        parts = [a + b for a, b in zip(parts[::2], parts[1::2])] + parts[len(parts) & ~1 :]
    return parts[0]


def factor(curv, lines, chores):
    full = (8, 128)
    lane, sub = iota(full, 1), iota(full, 0)
    rows = [curv[8 * k : 8 * k + 8, :] for k in range(16)]
    lower, scaled = [], []
    for k in range(16):
        panel = rows[k]
        cols = [jnp.broadcast_to(panel[:, 8 * k + j : 8 * k + j + 1], full) for j in range(8)]
        for j in range(8):
            lines[k, j] = cols[j]
        held = {}
        for j in range(8):
            for i in range(j + 1):
                held[i, j] = jnp.broadcast_to(lines[k, j, i : i + 1, :], full)

        def at(i, j):
            return held[min(i, j), max(i, j)]

        for t in range(0, 8, 2):
            a, b, d = at(t, t), at(t, t + 1), at(t + 1, t + 1)
            det = 1.0 / (a * d - b * b)
            rest = [i for i in range(8) if i not in (t, t + 1)]
            one = {i: at(i, t) for i in rest}
            two = {i: at(i, t + 1) for i in rest}
            new_one = {i: (d * one[i] - b * two[i]) * det for i in rest}
            new_two = {i: (a * two[i] - b * one[i]) * det for i in rest}
            for j in rest:
                for i in rest:
                    if i <= j:
                        held[i, j] = held[i, j] - (one[i] * new_one[j] + two[i] * new_two[j])
            for i in rest:
                held[min(i, t), max(i, t)] = new_one[i]
                held[min(i, t + 1), max(i, t + 1)] = new_two[i]
            held[t, t], held[t, t + 1], held[t + 1, t + 1] = -d * det, b * det, -a * det
        columns = []
        for u in range(8):
            layer = [at(i, u) for i in range(8)]
            for bit in (1, 2, 4):
                layer = [
                    jnp.where((sub & bit) == 0, low, high) for low, high in zip(layer[::2], layer[1::2])
                ]
            columns.append(layer[0])
        inside = (lane // 8) == k
        panel = jnp.where(inside, jnp.where(lane % 8 == sub, 1.0, 0.0), panel)
        lower.append(jnp.where(lane < 8 * k + 8, panel, 0.0))
        panel = -total_of([columns[u] * panel[u : u + 1, :] for u in range(8)])
        spread = [jnp.broadcast_to(panel[u : u + 1, :], full) for u in range(8)]
        for o in range(k + 1, 16):
            was = rows[o]
            parts = [
                jnp.broadcast_to(was[:, 8 * k + u : 8 * k + u + 1], full) * spread[u] for u in range(8)
            ]
            rows[o] = jnp.where(inside, 0.0, was) - total_of(parts)
        scaled.append(jnp.where(lane < 8 * k + 8, panel, 0.0))
        for chore in chores[k]:
            chore()
    return jnp.concatenate(lower, axis=0), jnp.concatenate(scaled, axis=0)


def pick_lanes(pieces):
    place = iota(pieces[0].shape, 1) // 32
    out = pieces[3]
    for b in (2, 1, 0):
        out = jnp.where(place == b, pieces[b], out)
    return out


def roll32(value, by):
    by %= 4
    return value if by == 0 else pltpu.roll(value, by * 32, 1)


def dot(left, right, precision=HI):
    return jnp.dot(left, right, precision=precision, preferred_element_type=F32)


def halves(value):
    high = value.astype(BF16)
    return high, (value - high.astype(F32)).astype(BF16)


def thirds(value):
    high = value.astype(BF16)
    rest = value - high.astype(F32)
    mid = rest.astype(BF16)
    return high, mid, (rest - mid.astype(F32)).astype(BF16)


def assemble_kernel(count, window, weight, resid, local, glob, out, *scratch):
    wv, rv, lv, gv, gp, vg, turned, up, fore, back, stack, matrix, lines, sems = scratch
    copies = [
        pltpu.make_async_copy(source, target, sems.at[n])
        for n, (source, target) in enumerate(((local, lv), (weight, wv), (resid, rv), (glob, gv)))
    ]
    for copy in copies:
        copy.start()
    for copy in copies[:3]:
        copy.wait()
    live = jnp.where(iota((1, 512), 1) < count[0], wv[...], 0.0)
    vb = jnp.transpose(jnp.broadcast_to(live, (128, 512)))
    rb = jnp.transpose(jnp.broadcast_to(rv[...], (128, 512)))
    slopes = lv[...]
    wlt = jnp.transpose(slopes) * live
    curv = dot(wlt, slopes)
    curv = curv + jnp.where(iota((128, 128), 0) == iota((128, 128), 1), 1.0, 0.0)
    copies[3].wait()

    def permute(h):
        r = slice(h * 32, h * 32 + 32)
        for x in range(4):
            first = gv[r, x * 256 : x * 256 + 128]
            second = gv[r, x * 256 + 128 : x * 256 + 256]
            even = pick_lanes([first, roll32(first, -1), roll32(second, 2), roll32(second, 1)])
            odd = pick_lanes([roll32(first, -1), roll32(first, 2), roll32(second, 1), second])
            for value, start in ((even, x * 128), (odd, 512 + x * 128)):
                cols = slice(start, start + 128)
                gp[r, cols] = value
                vg[r, cols] = value * vb[r]

    def turn(k, c):
        cols = slice(c * 128, c * 128 + 128)
        high, low = halves(jnp.transpose(gp[k * 128 : k * 128 + 128, cols]))
        for place, value in enumerate((high, high, low)):
            turned[cols, place * 512 + k * 128 : place * 512 + k * 128 + 128] = value

    def couple(c):
        cols = slice(c * 256, c * 256 + 256)
        up[:, cols] = dot(wlt, gp[:, cols])

    chores = [[] for _ in range(16)]
    for h in range(16):
        chores[h // 2].append(functools.partial(permute, h))
    for c in range(8):
        for k in range(4):
            chores[8 + c].append(functools.partial(turn, k, c))
    for c in range(4):
        chores[8 + 2 * c].append(functools.partial(couple, c))
    wl = jnp.transpose(wlt)
    lower, scaled = factor(curv, lines, chores)

    forward = lax.dot_general(
        wl, lower, (((1,), (1,)), ((), ())), precision=HI, preferred_element_type=F32
    )
    high, mid, low = thirds(forward)
    for place, value in enumerate((high, high, mid, mid, high, low)):
        fore[:, place * 128 : place * 128 + 128] = value
    for c in range(4):
        cols = slice(c * 256, c * 256 + 256)
        high, mid, low = thirds(dot(scaled, up[:, cols]))
        for place, value in enumerate((high, mid, high, mid, low, high)):
            back[place * 128 : place * 128 + 128, cols] = value

    for c in range(4):
        cols = slice(c * 256, c * 256 + 256)
        gv[:, cols] = dot(fore[...], back[:, cols], None)
    rhs = []
    for c in range(8):
        cols = slice(c * 128, c * 128 + 128)
        left = vg[:, cols] - gv[:, cols]
        rhs.append(jnp.sum(left * rb, axis=0, keepdims=True))
        high, low = halves(left)
        for place, value in enumerate((high, low, high)):
            stack[place * 512 : place * 512 + 512, cols] = value

    for q in range(2):
        for jh in range(2):
            n = slice((q * 2 + jh) * 256, (q * 2 + jh) * 256 + 256)
            for p in range(2):
                for ih in range(2):
                    if (p == q and ih > jh) or (p != q and ih < jh):
                        continue
                    m = slice((p * 2 + ih) * 256, (p * 2 + ih) * 256 + 256)
                    matrix[m, n] = dot(turned[m, :], stack[:, n], None)

    place = iota((32, 128), 1) // 32
    below = iota((32, 128), 0) >= iota((32, 128), 1) % 32
    ondiag = iota((32, 128), 0) == iota((32, 128), 1) % 32
    sub8 = iota((8, 128), 0)
    own = jnp.broadcast_to(window[0].astype(F32), (8, 128))
    for x in range(4):
        for y in range(4):
            i = x * 4 + y
            pair = matrix[512 + i * 32 : 512 + i * 32 + 32, x * 128 : x * 128 + 128]
            held = jnp.where(ondiag & (place == y), pair, 0.0)
            edge = roll32(jnp.sum(held, axis=0, keepdims=True), -y)
            tails = []
            for b in range(2):
                sums = pick_lanes(
                    [
                        roll32(rhs[p * 4 + a * 2 + b], p * 2 + a - y)
                        for p in range(2)
                        for a in range(2)
                    ]
                )
                tails.append(jnp.where(sub8 == 0, sums, jnp.where(sub8 == 1, edge, own)))
            for q in range(2):
                dest = ((x * 4 + y) * 2 + q) * 2
                cols = slice(q * 512 + x * 128, q * 512 + x * 128 + 128)
                for z in range(4):
                    i = z * 4 + y
                    same = slice(q * 512 + i * 32, q * 512 + i * 32 + 32)
                    cross = slice((1 - q) * 512 + i * 32, (1 - q) * 512 + i * 32 + 32)
                    if i < x * 4:
                        tile = matrix[same, cols]
                    elif i > x * 4 + 3:
                        tile = matrix[cross, cols]
                    else:
                        j = place + x * 4
                        tile = jnp.where(
                            (j > i) | ((j == i) & below), matrix[same, cols], matrix[cross, cols]
                        )
                    out[dest + z % 2, z // 2 * 32 : z // 2 * 32 + 32, :] = tile
                for b in range(2):
                    out[dest + b, 64:72, :] = tails[b]


def windows_kernel(arrived, out):
    def sums(g):
        acc = [jnp.zeros((8, 128), F32) for _ in range(NWIN)]
        for s in range(64):
            block = arrived[s, pl.ds(g * 8, 8), :]
            which = jnp.broadcast_to(arrived[s, 66:67, :], (8, 128))
            for w in range(NWIN):
                acc[w] = acc[w] + jnp.where(which == float(w), block, 0.0)
        return acc

    def packed(acc, back):
        return pick_lanes([roll32(acc[w], w - back) for w in range(NWIN)])

    @pl.loop(0, 2)
    def _(a):
        for k in range(4):
            acc = sums(a * 4 + k)
            for h in range(4):
                out[h * 2 + a, k * 8 : k * 8 + 8, :] = packed(acc, h)

    acc = sums(8)
    sub = iota((8, 128), 0)
    edge = jnp.broadcast_to(packed(acc, 0)[1:2, :], (8, 128))
    for a in range(2):
        first = jnp.broadcast_to(packed(acc, a)[0:1, :], (8, 128))
        second = jnp.broadcast_to(packed(acc, 2 + a)[0:1, :], (8, 128))
        tail = jnp.where(sub == 0, first, jnp.where(sub == 1, second, edge))
        for h in range(4):
            out[h * 2 + a, 32:40, :] = tail


def ring_kernel(arrived, out):
    total = arrived[0]
    for s in range(1, 8):
        total = total + arrived[s]
    out[...] = total


def finish_kernel(mine, other, out, rhs):
    x, zh, q = lax.axis_index("wide_0"), lax.axis_index("wide_1"), lax.axis_index("wide_2")
    zl = lax.axis_index("narrow_0") * 2 + lax.axis_index("narrow_1")
    y = lax.axis_index("narrow_2")
    i, j = zl * 4 + y, x * 4 + zh
    diag = jnp.broadcast_to(i == j, (32, 32))
    half = jnp.where(i <= j, q, 1 - q)
    lower = jnp.broadcast_to(half == 0, (32, 32))
    a, b = iota((32, 32), 0), iota((32, 32), 1)
    turned = jnp.transpose(mine[0:32, :])
    for w in range(NWIN):
        cols = slice(w * 32, w * 32 + 32)
        held, theirs = mine[0:32, cols], other[0:32, cols]
        flip = turned[cols, :]
        edge = jnp.broadcast_to(mine[34:35, cols], (32, 32))
        own_part = jnp.where(diag & (a >= b), held, flip)
        other_part = jnp.where(diag & (a == b), edge, jnp.where(diag & (a > b), flip, theirs))
        out[w, :, 0:32] = jnp.where(lower, own_part, other_part)
        out[w, :, 32:64] = jnp.where(lower, other_part, own_part)
        rhs[w : w + 1, 0:32] = mine[32:33, cols]
        rhs[w : w + 1, 32:64] = mine[33:34, cols]


def vmem(count):
    return [pl.BlockSpec(memory_space=pltpu.VMEM)] * count


def turn_pairs():
    place = lambda x, zh, q, zl, y: (((x * 4 + zh) * 2 + q) * 4 + zl) * 4 + y
    pairs = []
    for x in range(4):
        for zh in range(4):
            for q in range(2):
                for zl in range(4):
                    for y in range(4):
                        i, j = zl * 4 + y, x * 4 + zh
                        p = q if i <= j else 1 - q
                        target = 1 - q if i == j else p
                        pairs.append((place(x, zh, q, zl, y), place(zl, y, target, x, zh)))
    return pairs


def on_device(local_slopes, global_slopes, residuals, weights, track_slot_count, windows):
    small = pltpu.CompilerParams(vmem_limit_bytes=8 << 20)
    big = pltpu.CompilerParams(vmem_limit_bytes=48 << 20)
    payload = pl.pallas_call(
        assemble_kernel,
        out_shape=jax.ShapeDtypeStruct((64, 72, 128), F32),
        in_specs=[pl.BlockSpec(memory_space=pltpu.SMEM)] * 2 + [pl.BlockSpec(memory_space=pltpu.HBM)] * 4,
        out_specs=vmem(1)[0],
        scratch_shapes=[
            pltpu.VMEM((1, 512), F32),
            pltpu.VMEM((1, 512), F32),
            pltpu.VMEM((512, 128), F32),
            pltpu.VMEM((512, 1024), F32),
            pltpu.VMEM((512, 1024), F32),
            pltpu.VMEM((512, 1024), F32),
            pltpu.VMEM((1024, 1536), BF16),
            pltpu.VMEM((128, 1024), F32),
            pltpu.VMEM((512, 768), BF16),
            pltpu.VMEM((768, 1024), BF16),
            pltpu.VMEM((1536, 1024), BF16),
            pltpu.VMEM((1024, 1024), F32),
            pltpu.VMEM((16, 8, 8, 128), F32),
            pltpu.SemaphoreType.DMA((4,)),
        ],
        compiler_params=big,
        name="assemble",
    )(
        track_slot_count,
        windows,
        *[
            pltpu.with_memory_space_constraint(value, pltpu.HBM)
            for value in (weights, residuals, local_slopes[0], global_slopes[0])
        ],
    )
    arrived = lax.all_to_all(payload, PLANE, split_axis=0, concat_axis=0, tiled=True)
    packed = pl.pallas_call(
        windows_kernel,
        out_shape=jax.ShapeDtypeStruct((8, 40, 128), F32),
        in_specs=vmem(1),
        out_specs=vmem(1)[0],
        compiler_params=big,
        name="window_sums",
    )(arrived)
    ring = lax.all_to_all(packed, RING, split_axis=0, concat_axis=0, tiled=True)
    mine = pl.pallas_call(
        ring_kernel,
        out_shape=jax.ShapeDtypeStruct((40, 128), F32),
        in_specs=vmem(1),
        out_specs=vmem(1)[0],
        compiler_params=small,
        name="ring_sums",
    )(ring)
    other = lax.ppermute(mine, AXES, turn_pairs())
    out, rhs = pl.pallas_call(
        finish_kernel,
        out_shape=(
            jax.ShapeDtypeStruct((NWIN, 32, 64), F32),
            jax.ShapeDtypeStruct((NWIN, 64), F32),
        ),
        in_specs=vmem(2),
        out_specs=tuple(vmem(2)),
        compiler_params=small,
        name="finish",
    )(mine, other)
    return jnp.transpose(out, (0, 2, 1)), rhs


def solution(mesh):
    split = Mesh(mesh.devices.reshape(4, 4, 2, 2, 2, 4), AXES)
    return jax.shard_map(
        on_device,
        mesh=split,
        in_specs=(
            P(AXES, None, None),
            P(AXES, None, None),
            P(AXES, None),
            P(AXES, None),
            P(AXES),
            P(AXES),
        ),
        out_specs=(
            P(None, NARROW, WIDE),
            P(None, NARROW),
        ),
        check_vma=False,
    )
```

```python
import functools

import jax
import jax.numpy as jnp
from jax import lax
from jax.experimental import pallas as pl
from jax.experimental.pallas import tpu as pltpu
from jax.sharding import Mesh
from jax.sharding import PartitionSpec as P

NWIN = 4
AXES = ("wide_0", "wide_1", "wide_2", "narrow_0", "narrow_1", "narrow_2")
NARROW = AXES[3:]
WIDE = AXES[:3]
PLANE = ("wide_0", "narrow_2", "wide_2", "narrow_1")
RING = ("wide_1", "narrow_0")
HI = lax.Precision.HIGHEST
F32 = jnp.float32
BF16 = jnp.bfloat16


def iota(shape, dim):
    return lax.broadcasted_iota(jnp.int32, shape, dim)


def total_of(parts):
    while len(parts) > 1:
        parts = [a + b for a, b in zip(parts[::2], parts[1::2])] + parts[len(parts) & ~1 :]
    return parts[0]


def factor(curv, lines, chores):
    full = (8, 128)
    lane, sub = iota(full, 1), iota(full, 0)
    rows = [curv[8 * k : 8 * k + 8, :] for k in range(16)]
    lower, scaled = [], []
    for k in range(16):
        panel = rows[k]
        cols = [jnp.broadcast_to(panel[:, 8 * k + j : 8 * k + j + 1], full) for j in range(8)]
        for j in range(8):
            lines[k, j] = cols[j]
        held = {}
        for j in range(8):
            for i in range(j + 1):
                held[i, j] = jnp.broadcast_to(lines[k, j, i : i + 1, :], full)

        def at(i, j):
            return held[min(i, j), max(i, j)]

        for t in range(0, 8, 2):
            a, b, d = at(t, t), at(t, t + 1), at(t + 1, t + 1)
            det = 1.0 / (a * d - b * b)
            rest = [i for i in range(8) if i not in (t, t + 1)]
            one = {i: at(i, t) for i in rest}
            two = {i: at(i, t + 1) for i in rest}
            new_one = {i: (d * one[i] - b * two[i]) * det for i in rest}
            new_two = {i: (a * two[i] - b * one[i]) * det for i in rest}
            for j in rest:
                for i in rest:
                    if i <= j:
                        held[i, j] = held[i, j] - (one[i] * new_one[j] + two[i] * new_two[j])
            for i in rest:
                held[min(i, t), max(i, t)] = new_one[i]
                held[min(i, t + 1), max(i, t + 1)] = new_two[i]
            held[t, t], held[t, t + 1], held[t + 1, t + 1] = -d * det, b * det, -a * det
        columns = []
        for u in range(8):
            layer = [at(i, u) for i in range(8)]
            for bit in (1, 2, 4):
                layer = [
                    jnp.where((sub & bit) == 0, low, high) for low, high in zip(layer[::2], layer[1::2])
                ]
            columns.append(layer[0])
        inside = (lane // 8) == k
        panel = jnp.where(inside, jnp.where(lane % 8 == sub, 1.0, 0.0), panel)
        lower.append(jnp.where(lane < 8 * k + 8, panel, 0.0))
        panel = -total_of([columns[u] * panel[u : u + 1, :] for u in range(8)])
        spread = [jnp.broadcast_to(panel[u : u + 1, :], full) for u in range(8)]
        for o in range(k + 1, 16):
            was = rows[o]
            parts = [
                jnp.broadcast_to(was[:, 8 * k + u : 8 * k + u + 1], full) * spread[u] for u in range(8)
            ]
            rows[o] = jnp.where(inside, 0.0, was) - total_of(parts)
        scaled.append(jnp.where(lane < 8 * k + 8, panel, 0.0))
        for chore in chores[k]:
            chore()
    return jnp.concatenate(lower, axis=0), jnp.concatenate(scaled, axis=0)


def pick_lanes(pieces):
    place = iota(pieces[0].shape, 1) // 32
    out = pieces[3]
    for b in (2, 1, 0):
        out = jnp.where(place == b, pieces[b], out)
    return out


def roll32(value, by):
    by %= 4
    return value if by == 0 else pltpu.roll(value, by * 32, 1)


def dot(left, right, precision=HI):
    return jnp.dot(left, right, precision=precision, preferred_element_type=F32)


def halves(value):
    high = value.astype(BF16)
    return high, (value - high.astype(F32)).astype(BF16)


def thirds(value):
    high = value.astype(BF16)
    rest = value - high.astype(F32)
    mid = rest.astype(BF16)
    return high, mid, (rest - mid.astype(F32)).astype(BF16)


def assemble_kernel(count, window, weight, resid, local, glob, out, *scratch):
    wv, rv, lv, gv, gp, vg, turned, up, fore, back, stack, matrix, lines, sems = scratch
    copies = [
        pltpu.make_async_copy(source, target, sems.at[n])
        for n, (source, target) in enumerate(((local, lv), (weight, wv), (resid, rv), (glob, gv)))
    ]
    for copy in copies:
        copy.start()
    for copy in copies[:3]:
        copy.wait()
    live = jnp.where(iota((1, 512), 1) < count[0], wv[...], 0.0)
    vb = jnp.transpose(jnp.broadcast_to(live, (128, 512)))
    rb = jnp.transpose(jnp.broadcast_to(rv[...], (128, 512)))
    slopes = lv[...]
    wlt = jnp.transpose(slopes) * live
    curv = dot(wlt, slopes)
    curv = curv + jnp.where(iota((128, 128), 0) == iota((128, 128), 1), 1.0, 0.0)
    copies[3].wait()

    def permute(h):
        r = slice(h * 32, h * 32 + 32)
        for x in range(4):
            first = gv[r, x * 256 : x * 256 + 128]
            second = gv[r, x * 256 + 128 : x * 256 + 256]
            even = pick_lanes([first, roll32(first, -1), roll32(second, 2), roll32(second, 1)])
            odd = pick_lanes([roll32(first, -1), roll32(first, 2), roll32(second, 1), second])
            for value, start in ((even, x * 128), (odd, 512 + x * 128)):
                cols = slice(start, start + 128)
                gp[r, cols] = value
                vg[r, cols] = value * vb[r]

    def turn(k, c):
        cols = slice(c * 128, c * 128 + 128)
        high, low = halves(jnp.transpose(gp[k * 128 : k * 128 + 128, cols]))
        for place, value in enumerate((high, high, low)):
            turned[cols, place * 512 + k * 128 : place * 512 + k * 128 + 128] = value

    def couple(c):
        cols = slice(c * 256, c * 256 + 256)
        up[:, cols] = dot(wlt, gp[:, cols])

    chores = [[] for _ in range(16)]
    for h in range(16):
        chores[h // 2].append(functools.partial(permute, h))
    for c in range(8):
        for k in range(4):
            chores[8 + c].append(functools.partial(turn, k, c))
    for c in range(4):
        chores[8 + 2 * c].append(functools.partial(couple, c))
    wl = jnp.transpose(wlt)
    lower, scaled = factor(curv, lines, chores)

    forward = lax.dot_general(
        wl, lower, (((1,), (1,)), ((), ())), precision=HI, preferred_element_type=F32
    )
    high, mid, low = thirds(forward)
    for place, value in enumerate((high, high, mid, mid, high, low)):
        fore[:, place * 128 : place * 128 + 128] = value
    for c in range(4):
        cols = slice(c * 256, c * 256 + 256)
        high, mid, low = thirds(dot(scaled, up[:, cols]))
        for place, value in enumerate((high, mid, high, mid, low, high)):
            back[place * 128 : place * 128 + 128, cols] = value

    rhs = []

    def solved(n):
        cols = slice(n * 256, n * 256 + 256)
        gv[:, cols] = dot(fore[...], back[:, cols], None)

    def subtract(n):
        for c in (2 * n, 2 * n + 1):
            cols = slice(c * 128, c * 128 + 128)
            left = vg[:, cols] - gv[:, cols]
            rhs.append(jnp.sum(left * rb, axis=0, keepdims=True))
            high, low = halves(left)
            for place, value in enumerate((high, low, high)):
                stack[place * 512 : place * 512 + 512, cols] = value

    def multiply(n):
        q, jh = n // 2, n % 2
        cols = slice(n * 256, n * 256 + 256)
        for p in range(2):
            for ih in range(2):
                if (p == q and ih > jh) or (p != q and ih < jh):
                    continue
                m = slice((p * 2 + ih) * 256, (p * 2 + ih) * 256 + 256)
                matrix[m, cols] = dot(turned[m, :], stack[:, cols], None)

    place = iota((32, 128), 1) // 32
    below = iota((32, 128), 0) >= iota((32, 128), 1) % 32
    ondiag = iota((32, 128), 0) == iota((32, 128), 1) % 32

    def pack(n):
        q = n // 2
        for x in (n % 2 * 2, n % 2 * 2 + 1):
            cols = slice(q * 512 + x * 128, q * 512 + x * 128 + 128)
            for y in range(4):
                dest = ((x * 4 + y) * 2 + q) * 2
                for z in range(4):
                    i = z * 4 + y
                    same = slice(q * 512 + i * 32, q * 512 + i * 32 + 32)
                    cross = slice((1 - q) * 512 + i * 32, (1 - q) * 512 + i * 32 + 32)
                    if i < x * 4:
                        tile = matrix[same, cols]
                    elif i > x * 4 + 3:
                        tile = matrix[cross, cols]
                    else:
                        j = place + x * 4
                        tile = jnp.where(
                            (j > i) | ((j == i) & below), matrix[same, cols], matrix[cross, cols]
                        )
                    out[dest + z % 2, z // 2 * 32 : z // 2 * 32 + 32, :] = tile

    solved(0)
    solved(1)
    subtract(0)
    for n in range(4):
        if n < 2:
            solved(n + 2)
        multiply(n)
        if n < 3:
            subtract(n + 1)
        if n > 0:
            pack(n - 1)
    pack(3)

    sub8 = iota((8, 128), 0)
    own = jnp.broadcast_to(window[0].astype(F32), (8, 128))
    for x in range(4):
        for y in range(4):
            i = x * 4 + y
            pair = matrix[512 + i * 32 : 512 + i * 32 + 32, x * 128 : x * 128 + 128]
            kept = jnp.where(ondiag & (place == y), pair, 0.0)
            edge = roll32(jnp.sum(kept, axis=0, keepdims=True), -y)
            for b in range(2):
                sums = pick_lanes(
                    [
                        roll32(rhs[p * 4 + a * 2 + b], p * 2 + a - y)
                        for p in range(2)
                        for a in range(2)
                    ]
                )
                tail = jnp.where(sub8 == 0, sums, jnp.where(sub8 == 1, edge, own))
                for q in range(2):
                    out[((x * 4 + y) * 2 + q) * 2 + b, 64:72, :] = tail


def windows_kernel(arrived, out):
    def sums(groups):
        acc = [[jnp.zeros((8, 128), F32) for _ in range(NWIN)] for _ in groups]
        for s in range(64):
            which = jnp.broadcast_to(arrived[s, 66:67, :], (8, 128))
            hits = [which == float(w) for w in range(NWIN)]
            for n, g in enumerate(groups):
                block = arrived[s, pl.ds(g * 8, 8), :]
                for w in range(NWIN):
                    acc[n][w] = acc[n][w] + jnp.where(hits[w], block, 0.0)
        return acc

    def packed(acc, back):
        return pick_lanes([roll32(acc[w], w - back) for w in range(NWIN)])

    @pl.loop(0, 2)
    def _(a):
        for k, acc in enumerate(sums([a * 4 + k for k in range(4)])):
            for h in range(4):
                out[h * 2 + a, k * 8 : k * 8 + 8, :] = packed(acc, h)

    (acc,) = sums([8])
    sub = iota((8, 128), 0)
    edge = jnp.broadcast_to(packed(acc, 0)[1:2, :], (8, 128))
    for a in range(2):
        first = jnp.broadcast_to(packed(acc, a)[0:1, :], (8, 128))
        second = jnp.broadcast_to(packed(acc, 2 + a)[0:1, :], (8, 128))
        tail = jnp.where(sub == 0, first, jnp.where(sub == 1, second, edge))
        for h in range(4):
            out[h * 2 + a, 32:40, :] = tail


def ring_kernel(arrived, out):
    total = arrived[0]
    for s in range(1, 8):
        total = total + arrived[s]
    out[...] = total


def finish_kernel(mine, other, out, rhs):
    x, zh, q = lax.axis_index("wide_0"), lax.axis_index("wide_1"), lax.axis_index("wide_2")
    zl = lax.axis_index("narrow_0") * 2 + lax.axis_index("narrow_1")
    y = lax.axis_index("narrow_2")
    i, j = zl * 4 + y, x * 4 + zh
    diag = jnp.broadcast_to(i == j, (32, 32))
    half = jnp.where(i <= j, q, 1 - q)
    lower = jnp.broadcast_to(half == 0, (32, 32))
    a, b = iota((32, 32), 0), iota((32, 32), 1)
    turned = jnp.transpose(mine[0:32, :])
    for w in range(NWIN):
        cols = slice(w * 32, w * 32 + 32)
        held, theirs = mine[0:32, cols], other[0:32, cols]
        flip = turned[cols, :]
        edge = jnp.broadcast_to(mine[34:35, cols], (32, 32))
        own_part = jnp.where(diag & (a >= b), held, flip)
        other_part = jnp.where(diag & (a == b), edge, jnp.where(diag & (a > b), flip, theirs))
        out[w, :, 0:32] = jnp.where(lower, own_part, other_part)
        out[w, :, 32:64] = jnp.where(lower, other_part, own_part)
        rhs[w : w + 1, 0:32] = mine[32:33, cols]
        rhs[w : w + 1, 32:64] = mine[33:34, cols]


def vmem(count):
    return [pl.BlockSpec(memory_space=pltpu.VMEM)] * count


def turn_pairs():
    place = lambda x, zh, q, zl, y: (((x * 4 + zh) * 2 + q) * 4 + zl) * 4 + y
    pairs = []
    for x in range(4):
        for zh in range(4):
            for q in range(2):
                for zl in range(4):
                    for y in range(4):
                        i, j = zl * 4 + y, x * 4 + zh
                        p = q if i <= j else 1 - q
                        target = 1 - q if i == j else p
                        pairs.append((place(x, zh, q, zl, y), place(zl, y, target, x, zh)))
    return pairs


def on_device(local_slopes, global_slopes, residuals, weights, track_slot_count, windows):
    small = pltpu.CompilerParams(vmem_limit_bytes=8 << 20)
    big = pltpu.CompilerParams(vmem_limit_bytes=48 << 20)
    payload = pl.pallas_call(
        assemble_kernel,
        out_shape=jax.ShapeDtypeStruct((64, 72, 128), F32),
        in_specs=[pl.BlockSpec(memory_space=pltpu.SMEM)] * 2 + [pl.BlockSpec(memory_space=pltpu.HBM)] * 4,
        out_specs=vmem(1)[0],
        scratch_shapes=[
            pltpu.VMEM((1, 512), F32),
            pltpu.VMEM((1, 512), F32),
            pltpu.VMEM((512, 128), F32),
            pltpu.VMEM((512, 1024), F32),
            pltpu.VMEM((512, 1024), F32),
            pltpu.VMEM((512, 1024), F32),
            pltpu.VMEM((1024, 1536), BF16),
            pltpu.VMEM((128, 1024), F32),
            pltpu.VMEM((512, 768), BF16),
            pltpu.VMEM((768, 1024), BF16),
            pltpu.VMEM((1536, 1024), BF16),
            pltpu.VMEM((1024, 1024), F32),
            pltpu.VMEM((16, 8, 8, 128), F32),
            pltpu.SemaphoreType.DMA((4,)),
        ],
        compiler_params=big,
        name="assemble",
    )(
        track_slot_count,
        windows,
        *[
            pltpu.with_memory_space_constraint(value, pltpu.HBM)
            for value in (weights, residuals, local_slopes[0], global_slopes[0])
        ],
    )
    arrived = lax.all_to_all(payload, PLANE, split_axis=0, concat_axis=0, tiled=True)
    packed = pl.pallas_call(
        windows_kernel,
        out_shape=jax.ShapeDtypeStruct((8, 40, 128), F32),
        in_specs=vmem(1),
        out_specs=vmem(1)[0],
        compiler_params=big,
        name="window_sums",
    )(arrived)
    ring = lax.all_to_all(packed, RING, split_axis=0, concat_axis=0, tiled=True)
    mine = pl.pallas_call(
        ring_kernel,
        out_shape=jax.ShapeDtypeStruct((40, 128), F32),
        in_specs=vmem(1),
        out_specs=vmem(1)[0],
        compiler_params=small,
        name="ring_sums",
    )(ring)
    other = lax.ppermute(mine, AXES, turn_pairs())
    out, rhs = pl.pallas_call(
        finish_kernel,
        out_shape=(
            jax.ShapeDtypeStruct((NWIN, 32, 64), F32),
            jax.ShapeDtypeStruct((NWIN, 64), F32),
        ),
        in_specs=vmem(2),
        out_specs=tuple(vmem(2)),
        compiler_params=small,
        name="finish",
    )(mine, other)
    return jnp.transpose(out, (0, 2, 1)), rhs


def solution(mesh):
    split = Mesh(mesh.devices.reshape(4, 4, 2, 2, 2, 4), AXES)
    return jax.shard_map(
        on_device,
        mesh=split,
        in_specs=(
            P(AXES, None, None),
            P(AXES, None, None),
            P(AXES, None),
            P(AXES, None),
            P(AXES),
            P(AXES),
        ),
        out_specs=(
            P(None, NARROW, WIDE),
            P(None, NARROW),
        ),
        check_vma=False,
    )
```
